32 devices in a mesh: seq: 8 (over y, x, core), ch: 4 (over z).
Axes of the slice: x: 2, y: 2, z: 4, core: 2. Of those that a mesh axis runs over, the one named last changes fastest.
Arguments:
- out_gate: bfloat16 [4096, 1024], P('ch', 'seq'), may hold values from -6 to 6
- key_proj: bfloat16 [4096, 1024], P('ch', 'seq'), may hold values from -6 to 6
- value_proj: bfloat16 [4096, 1024], P('ch', 'seq'), may hold values from -6 to 6
- long_filter: bfloat16 [4096, 1024], P('ch', 'seq'), may hold values from -0.1875 to 0.1875
- skip_gain: float32 [4096], P('ch'), may hold values from -4 to 4
- residual: bfloat16 [4096, 1024], P('ch', 'seq'), may hold values from -6 to 6
- norm_gain: float32 [4096], P('ch'), may hold values from 0.5 to 1.5
Outputs:
- mixed: bfloat16 [4096, 1024], P('ch', 'seq')
- normed: bfloat16 [4096, 1024], P('ch', 'seq')
The draws below stay inside these ranges and needn't reach their ends.
All inputs are finite; a program needn't handle non-finite values.
Results may differ from the reference program's by a relative error of at most 0.0075.
Values may be sent and summed in bfloat16 or wider, within the bound.
A program may use at most 64 MiB of HBM per device.

```python
import jax
import jax.numpy as jnp
from jax import lax

D = 4096
SEQ = 1024


def block_levels(rng, extent, split, least, high):
    factor_of, own = 1.0, jax.random.fold_in(rng, 6)
    for position, shards_of in split:
        draws = jnp.exp(jax.random.uniform(jax.random.fold_in(own, position), (shards_of,), jnp.float32, least / len(split), high / len(split)))
        factor_of = factor_of * jnp.repeat(draws, extent[position] // shards_of).reshape([-1 if axis == position else 1 for axis in range(len(extent))])
    return factor_of


def centred(own_key, dims, width, limit, shards=(), kind=jnp.bfloat16):
    drawn = jax.random.normal(own_key, dims, jnp.float32) * width
    if len(shards) > 0:
        drawn = block_levels(own_key, dims, shards, -0.22, 0.18) * drawn
    return jnp.clip(drawn, min=-limit, max=limit).astype(kind)


def setup_inputs(seed: int = 0) -> dict:
    key_of = jax.random.split(jax.random.key(seed), 8)
    return {
        "out_gate": centred(key_of[0], (D, SEQ), 1.0, 6.0, ((0, 4), (1, 8))),
        "key_proj": centred(key_of[1], (D, SEQ), 1.0, 6.0, ((0, 4), (1, 8))),
        "value_proj": centred(key_of[2], (D, SEQ), 1.0, 6.0, ((0, 4), (1, 8))),
        "long_filter": centred(key_of[3], (D, SEQ), SEQ ** -0.5, 0.1875, ((0, 4), (1, 8))),
        "skip_gain": centred(key_of[4], (D,), 1.0, 4.0, ((0, 4),), jnp.float32),
        "residual": centred(key_of[5], (D, SEQ), 1.0, 6.0, ((0, 4), (1, 8))),
        "norm_gain": jnp.clip(1.0 + 0.1 * jax.random.normal(key_of[6], (D,), jnp.float32), 0.5, 1.5),
    }


def reference(out_gate, key_proj, value_proj, long_filter, skip_gain, residual, norm_gain):
    product_in = (key_proj.astype(jnp.float32) * value_proj.astype(jnp.float32)).astype(jnp.bfloat16)
    group_width = 64
    groups = D // group_width

    def one_group(pieces):
        signal, kernel, gate_rows, skip_rows, stream_rows = pieces
        signal_f = signal.astype(jnp.float32)
        length = signal_f.shape[1]
        spectrum = jnp.fft.rfft(signal_f, n=2 * length, axis=1) * jnp.fft.rfft(kernel.astype(jnp.float32), n=2 * length, axis=1)
        convolved = jnp.fft.irfft(spectrum, n=2 * length, axis=1)[:, :length].astype(signal_f.dtype)
        return stream_rows.astype(jnp.float32) + gate_rows.astype(jnp.float32) * (convolved + skip_rows[:, None] * signal_f)
    total = lax.map(one_group, (product_in.reshape(groups, group_width, -1), long_filter.reshape(groups, group_width, -1), out_gate.reshape(groups, group_width, -1), skip_gain.reshape(groups, group_width), residual.reshape(groups, group_width, -1)))
    total = total.reshape(D, -1)
    mixed = total.astype(jnp.bfloat16)
    mean_square = lax.optimization_barrier(jnp.mean(total * total, axis=0))
    normed = (total * lax.rsqrt(mean_square + 1e-06)[None, :] * norm_gain[:, None]).astype(jnp.bfloat16)
    return (mixed, normed)
```

```python
import math

import numpy as np

import jax
import jax.numpy as jnp
from jax import lax
from jax.experimental import pallas as pl
from jax.experimental.pallas import tpu as pltpu
from jax.sharding import PartitionSpec as P

D = 4096


HIGHEST = lax.Precision.HIGHEST


def tables(count, span, period):
    row_ids = jnp.arange(count, dtype=jnp.int32)[:, None]
    col_ids = jnp.arange(span, dtype=jnp.int32)[None, :]
    phases = (row_ids * col_ids % period).astype(jnp.float32) * (2.0 * math.pi / period)
    return (jnp.cos(phases), jnp.sin(phases))


def product(left, right):
    return jnp.dot(left, right, precision=HIGHEST, preferred_element_type=jnp.float32)


def block_spectrum(signal):
    width = signal.shape[1]
    cosine, sine = tables(width, 2 * width, 2 * width)
    return (product(signal, cosine), -product(signal, sine))


def block_inverse(real_part, imag_part):
    span = real_part.shape[1]
    cosine, sine = tables(span, span, span)
    return (product(real_part, cosine) - product(imag_part, sine)) / span


def index_convolve(input_real, input_imag, filter_real, filter_imag):
    blocks = input_real.shape[0]
    forward_cos, forward_sin = tables(2 * blocks, blocks, 2 * blocks)

    def forward(real_part, imag_part):
        return (
            product(forward_cos, real_part) + product(forward_sin, imag_part),
            product(forward_cos, imag_part) - product(forward_sin, real_part),
        )

    signal_real, signal_imag = forward(input_real, input_imag)
    kernel_real, kernel_imag = forward(filter_real, filter_imag)
    joint_real = signal_real * kernel_real - signal_imag * kernel_imag
    joint_imag = signal_real * kernel_imag + signal_imag * kernel_real
    back_cos, back_sin = tables(blocks, 2 * blocks, 2 * blocks)
    result_real = (product(back_cos, joint_real) - product(back_sin, joint_imag)) / (2 * blocks)
    result_imag = (product(back_cos, joint_imag) + product(back_sin, joint_real)) / (2 * blocks)
    return (result_real, result_imag)


def on_device(out_gate, key_proj, value_proj, long_filter, skip_gain, residual, norm_gain):
    chans, width = key_proj.shape
    blocks = lax.axis_size("seq")
    product_in = (key_proj.astype(jnp.float32) * value_proj.astype(jnp.float32)).astype(
        jnp.bfloat16
    )
    signal_f = product_in.astype(jnp.float32)
    whole_in, whole_filter = (
        lax.all_to_all(product_in, "seq", split_axis=0, concat_axis=1, tiled=True),
        lax.all_to_all(long_filter, "seq", split_axis=0, concat_axis=1, tiled=True),
    )
    group = whole_in.shape[0]

    def by_block(array):
        return (
            array.astype(jnp.float32)
            .reshape(group, blocks, width)
            .transpose(1, 0, 2)
            .reshape(blocks * group, width)
        )

    signal_real, signal_imag = block_spectrum(by_block(whole_in))
    kernel_real, kernel_imag = block_spectrum(by_block(whole_filter))
    result_real, result_imag = index_convolve(
        signal_real.reshape(blocks, -1),
        signal_imag.reshape(blocks, -1),
        kernel_real.reshape(blocks, -1),
        kernel_imag.reshape(blocks, -1),
    )
    timeline = block_inverse(
        result_real.reshape(blocks * group, 2 * width),
        result_imag.reshape(blocks * group, 2 * width),
    ).reshape(blocks, group, 2 * width)
    upper = timeline[:, :, width:]
    carried = jnp.concatenate([jnp.zeros((1, group, width), jnp.float32), upper[:-1]], axis=0)
    whole_out = (timeline[:, :, :width] + carried).transpose(1, 0, 2).reshape(group, blocks * width)
    convolved = lax.all_to_all(whole_out, "seq", split_axis=1, concat_axis=0, tiled=True)
    total = residual.astype(jnp.float32) + out_gate.astype(jnp.float32) * (
        convolved + skip_gain[:, None] * signal_f
    )
    squares = lax.psum(jnp.sum(total * total, axis=0), "ch")
    normed = total * lax.rsqrt(squares / D + 1e-06)[None, :] * norm_gain[:, None]
    return (total.astype(jnp.bfloat16), normed.astype(jnp.bfloat16))


CHUNKS = 2


def spectral_tables(width):
    n = np.arange(width)[:, None]
    k = np.arange(width)[None, :]
    angle = 2.0 * np.pi * (2 * k + 1) * n / (4 * width)
    forward = np.concatenate([np.cos(angle), -np.sin(angle)], axis=1)
    inverse = forward.T / width

    def split(table):
        high = table.astype(jnp.bfloat16)
        low = (table - high.astype(np.float64)).astype(jnp.bfloat16)
        return high, low

    return (
        np.concatenate(split(forward), axis=0),
        np.concatenate(split(inverse), axis=1),
    )


def fused(
    key_hbm, value_hbm, filter_hbm, gate_hbm, residual_hbm, skip_ref, gain_ref, forward_ref, inverse_ref,
    mixed_ref, normed_ref,
    key_v, value_v, gate_v, residual_v, product_v, signal_in, filter_in, signal_spec, filter_spec, joint,
    back_out, back_in, total_v, squares_v, load_sem, send_sem, recv_sem, back_send, back_recv, sq_send, sq_recv,
):
    blocks, group, width = key_hbm.shape
    me = lax.axis_index("seq")
    lane = lax.axis_index("ch")
    lanes = squares_v.shape[0]
    rows = group // CHUNKS

    loads = [
        pltpu.make_async_copy(source, target, load_sem.at[i])
        for i, (source, target) in enumerate(
            ((key_hbm, key_v), (value_hbm, value_v), (filter_hbm.at[me], filter_in.at[me]),
             (gate_hbm, gate_v), (residual_hbm, residual_v))
        )
    ]
    for load in loads:
        load.start()
    barrier = pltpu.get_barrier_semaphore()
    for step in range(1, lanes):
        pl.semaphore_signal(barrier, inc=1, device_id={"ch": lax.rem(lane + step, lanes)})
    for step in range(1, blocks):
        pl.semaphore_signal(barrier, inc=1, device_id={"seq": lax.rem(me + step, blocks)})
    loads[0].wait()
    loads[1].wait()
    product_v[...] = (key_v[...].astype(jnp.float32) * value_v[...].astype(jnp.float32)).astype(jnp.bfloat16)
    pl.semaphore_wait(barrier, blocks - 1 + lanes - 1)

    def outbound(kind, chunk, step):
        peer = lax.rem(me + step, blocks)
        source, target = ((filter_hbm, filter_in), (product_v, signal_in))[kind]
        span = pl.ds(chunk * rows, rows)
        return pltpu.make_async_remote_copy(
            src_ref=source.at[peer, span],
            dst_ref=target.at[me, span],
            send_sem=send_sem.at[kind, chunk, step],
            recv_sem=recv_sem.at[kind, chunk, step],
            device_id={"seq": peer},
        )

    def inbound(kind, chunk, step):
        origin = lax.rem(me + blocks - step, blocks)
        target = (filter_in, signal_in)[kind]
        span = pl.ds(chunk * rows, rows)
        return pltpu.make_async_remote_copy(
            src_ref=target.at[origin, span],
            dst_ref=target.at[origin, span],
            send_sem=send_sem.at[kind, chunk, step],
            recv_sem=recv_sem.at[kind, chunk, step],
            device_id={"seq": origin},
        )

    def returning(chunk, step):
        peer = lax.rem(me + step, blocks)
        span = pl.ds(chunk * rows, rows)
        return pltpu.make_async_remote_copy(
            src_ref=back_out.at[peer, span],
            dst_ref=back_in.at[me, span],
            send_sem=back_send.at[chunk, step],
            recv_sem=back_recv.at[chunk, step],
            device_id={"seq": peer},
        )

    def returned(chunk, step):
        origin = lax.rem(me + blocks - step, blocks)
        span = pl.ds(chunk * rows, rows)
        return pltpu.make_async_remote_copy(
            src_ref=back_in.at[origin, span],
            dst_ref=back_in.at[origin, span],
            send_sem=back_send.at[chunk, step],
            recv_sem=back_recv.at[chunk, step],
            device_id={"seq": origin},
        )

    for chunk in range(CHUNKS):
        for kind in range(2):
            for step in range(1, blocks):
                outbound(kind, chunk, step).start()

    signal_in[me] = product_v[me]
    loads[2].wait()
    loads[3].wait()
    loads[4].wait()
    for b in range(blocks):
        skip = jnp.transpose(jnp.broadcast_to(skip_ref[b : b + 1, :], (width, group)))
        total_v[b] = residual_v[b].astype(jnp.float32) + gate_v[b].astype(jnp.float32) * (
            skip * product_v[b].astype(jnp.float32)
        )

    sign = (1 - 2 * (lax.broadcasted_iota(jnp.int32, (8, width), 1) % 2)).astype(jnp.float32)

    def spectrum(ref, chunk, out_ref):
        part = ref[:, chunk * rows : (chunk + 1) * rows, :].reshape(blocks * rows, width)
        doubled = jnp.concatenate([part, part], axis=1)
        out_ref[...] = jnp.dot(doubled, forward_ref[...], preferred_element_type=jnp.float32).reshape(
            blocks, rows, 2 * width
        )

    for chunk in range(CHUNKS):
        for step in range(1, blocks):
            inbound(0, chunk, step).wait_recv()
        spectrum(filter_in, chunk, filter_spec)
        for step in range(1, blocks):
            inbound(1, chunk, step).wait_recv()
        spectrum(signal_in, chunk, signal_spec)

        def one_octet(octet, carry):
            span = pl.ds(pl.multiple_of(octet * 8, 8), 8)
            plain_r = [signal_spec[b, span, :width] for b in range(blocks)]
            plain_i = [signal_spec[b, span, width:] for b in range(blocks)]
            input_r, input_i = [plain_r[0]], [plain_i[0]]
            for b in range(1, blocks):
                input_r.append(plain_r[b] - sign * plain_i[b - 1])
                input_i.append(plain_i[b] + sign * plain_r[b - 1])
            taps_r = [filter_spec[b, span, :width] for b in range(blocks)]
            taps_i = [filter_spec[b, span, width:] for b in range(blocks)]
            for j in range(blocks):
                real = taps_r[0] * input_r[j] - taps_i[0] * input_i[j]
                imag = taps_r[0] * input_i[j] + taps_i[0] * input_r[j]
                for d in range(1, j + 1):
                    real = real + taps_r[d] * input_r[j - d] - taps_i[d] * input_i[j - d]
                    imag = imag + taps_r[d] * input_i[j - d] + taps_i[d] * input_r[j - d]
                joint[j, span, :width] = real
                joint[j, span, width:] = imag
            return carry

        lax.fori_loop(0, rows // 8, one_octet, 0)
        timeline = jnp.dot(
            joint[...].reshape(blocks * rows, 2 * width).astype(jnp.bfloat16),
            inverse_ref[...],
            preferred_element_type=jnp.float32,
        )
        timeline = (timeline[:, :width] + timeline[:, width:]).astype(jnp.bfloat16)
        back_out[:, chunk * rows : (chunk + 1) * rows, :] = timeline.reshape(blocks, rows, width)
        for step in range(1, blocks):
            returning(chunk, step).start()
    back_in[me] = back_out[me]

    squares = jnp.zeros((8, width), jnp.float32)
    for chunk in range(CHUNKS):
        for step in range(1, blocks):
            returned(chunk, step).wait_recv()
        for b in range(blocks):
            span = pl.ds(chunk * rows, rows)
            total = total_v[b, span] + gate_v[b, span].astype(jnp.float32) * back_in[b, span].astype(jnp.float32)
            total_v[b, span] = total
            squares = squares + jnp.sum((total * total).reshape(rows // 8, 8, width), axis=0)
    squares_v[lane] = squares

    def share(step, other):
        return pltpu.make_async_remote_copy(
            src_ref=squares_v.at[other[0]],
            dst_ref=squares_v.at[other[0]],
            send_sem=sq_send.at[step],
            recv_sem=sq_recv.at[step],
            device_id={"ch": other[1]},
        )

    for step in range(1, lanes):
        share(step, (lane, lax.rem(lane + step, lanes))).start()
    mixed_ref[...] = total_v[...].astype(jnp.bfloat16)
    for step in range(1, lanes):
        origin = lax.rem(lane + lanes - step, lanes)
        share(step, (origin, origin)).wait_recv()
    everyone = jnp.sum(jnp.sum(squares_v[...], axis=0), axis=0, keepdims=True)
    scale = lax.rsqrt(everyone / (lanes * blocks * group) + 1e-06)
    for b in range(blocks):
        gain = jnp.transpose(jnp.broadcast_to(gain_ref[b : b + 1, :], (width, group)))
        normed_ref[b] = (total_v[b] * scale * gain).astype(jnp.bfloat16)

    for chunk in range(CHUNKS):
        for step in range(1, blocks):
            outbound(0, chunk, step).wait_send()
            outbound(1, chunk, step).wait_send()
            returning(chunk, step).wait_send()
    for step in range(1, lanes):
        share(step, (lane, lax.rem(lane + step, lanes))).wait_send()


def with_kernel(out_gate, key_proj, value_proj, long_filter, skip_gain, residual, norm_gain):
    chans, width = key_proj.shape
    blocks, lanes = lax.axis_size("seq"), lax.axis_size("ch")
    group = chans // blocks
    rows = group // CHUNKS
    shape = (blocks, group, width)
    forward, inverse = spectral_tables(width)
    bf16, f32 = jnp.bfloat16, jnp.float32
    anywhere = pl.BlockSpec(memory_space=pl.ANY)
    local = pl.BlockSpec(memory_space=pltpu.VMEM)
    dma = pltpu.SemaphoreType.DMA
    mixed, normed = pl.pallas_call(
        fused,
        out_shape=(jax.ShapeDtypeStruct(shape, bf16), jax.ShapeDtypeStruct(shape, bf16)),
        in_specs=[anywhere] * 5 + [local] * 4,
        out_specs=(local, local),
        scratch_shapes=[
            *[pltpu.VMEM(shape, bf16) for _ in range(7)],
            *[pltpu.VMEM((blocks, rows, 2 * width), f32) for _ in range(3)],
            pltpu.VMEM(shape, bf16),
            pltpu.VMEM(shape, bf16),
            pltpu.VMEM(shape, f32),
            pltpu.VMEM((lanes, 8, width), f32),
            dma((5,)),
            dma((2, CHUNKS, blocks)),
            dma((2, CHUNKS, blocks)),
            dma((CHUNKS, blocks)),
            dma((CHUNKS, blocks)),
            dma((lanes,)),
            dma((lanes,)),
        ],
        compiler_params=pltpu.CompilerParams(collective_id=0, has_side_effects=True),
    )(
        key_proj.reshape(shape),
        value_proj.reshape(shape),
        long_filter.reshape(shape),
        out_gate.reshape(shape),
        residual.reshape(shape),
        skip_gain.reshape(blocks, group),
        norm_gain.reshape(blocks, group),
        jnp.asarray(forward),
        jnp.asarray(inverse),
    )
    return mixed.reshape(chans, width), normed.reshape(chans, width)


def choose(out_gate, key_proj, *rest):
    chans, width = key_proj.shape
    blocks = lax.axis_size("seq")
    tiled = chans % (blocks * CHUNKS * 16) == 0 and width % 128 == 0 and blocks <= 16
    return (with_kernel if tiled else on_device)(out_gate, key_proj, *rest)


def solution(mesh):
    return jax.shard_map(
        choose,
        mesh=mesh,
        in_specs=(
            P("ch", "seq"),
            P("ch", "seq"),
            P("ch", "seq"),
            P("ch", "seq"),
            P("ch"),
            P("ch", "seq"),
            P("ch"),
        ),
        out_specs=(P("ch", "seq"), P("ch", "seq")),
        check_vma=False,
    )
```

```python
import math

import numpy as np

import jax
import jax.numpy as jnp
from jax import lax
from jax.experimental import pallas as pl
from jax.experimental.pallas import tpu as pltpu
from jax.sharding import PartitionSpec as P

D = 4096


HIGHEST = lax.Precision.HIGHEST


def tables(count, span, period):
    row_ids = jnp.arange(count, dtype=jnp.int32)[:, None]
    col_ids = jnp.arange(span, dtype=jnp.int32)[None, :]
    phases = (row_ids * col_ids % period).astype(jnp.float32) * (2.0 * math.pi / period)
    return (jnp.cos(phases), jnp.sin(phases))


def product(left, right):
    return jnp.dot(left, right, precision=HIGHEST, preferred_element_type=jnp.float32)


def block_spectrum(signal):
    width = signal.shape[1]
    cosine, sine = tables(width, 2 * width, 2 * width)
    return (product(signal, cosine), -product(signal, sine))


def block_inverse(real_part, imag_part):
    span = real_part.shape[1]
    cosine, sine = tables(span, span, span)
    return (product(real_part, cosine) - product(imag_part, sine)) / span


def index_convolve(input_real, input_imag, filter_real, filter_imag):
    blocks = input_real.shape[0]
    forward_cos, forward_sin = tables(2 * blocks, blocks, 2 * blocks)

    def forward(real_part, imag_part):
        return (
            product(forward_cos, real_part) + product(forward_sin, imag_part),
            product(forward_cos, imag_part) - product(forward_sin, real_part),
        )

    signal_real, signal_imag = forward(input_real, input_imag)
    kernel_real, kernel_imag = forward(filter_real, filter_imag)
    joint_real = signal_real * kernel_real - signal_imag * kernel_imag
    joint_imag = signal_real * kernel_imag + signal_imag * kernel_real
    back_cos, back_sin = tables(blocks, 2 * blocks, 2 * blocks)
    result_real = (product(back_cos, joint_real) - product(back_sin, joint_imag)) / (2 * blocks)
    result_imag = (product(back_cos, joint_imag) + product(back_sin, joint_real)) / (2 * blocks)
    return (result_real, result_imag)


def on_device(out_gate, key_proj, value_proj, long_filter, skip_gain, residual, norm_gain):
    chans, width = key_proj.shape
    blocks = lax.axis_size("seq")
    product_in = (key_proj.astype(jnp.float32) * value_proj.astype(jnp.float32)).astype(
        jnp.bfloat16
    )
    signal_f = product_in.astype(jnp.float32)
    whole_in, whole_filter = (
        lax.all_to_all(product_in, "seq", split_axis=0, concat_axis=1, tiled=True),
        lax.all_to_all(long_filter, "seq", split_axis=0, concat_axis=1, tiled=True),
    )
    group = whole_in.shape[0]

    def by_block(array):
        return (
            array.astype(jnp.float32)
            .reshape(group, blocks, width)
            .transpose(1, 0, 2)
            .reshape(blocks * group, width)
        )

    signal_real, signal_imag = block_spectrum(by_block(whole_in))
    kernel_real, kernel_imag = block_spectrum(by_block(whole_filter))
    result_real, result_imag = index_convolve(
        signal_real.reshape(blocks, -1),
        signal_imag.reshape(blocks, -1),
        kernel_real.reshape(blocks, -1),
        kernel_imag.reshape(blocks, -1),
    )
    timeline = block_inverse(
        result_real.reshape(blocks * group, 2 * width),
        result_imag.reshape(blocks * group, 2 * width),
    ).reshape(blocks, group, 2 * width)
    upper = timeline[:, :, width:]
    carried = jnp.concatenate([jnp.zeros((1, group, width), jnp.float32), upper[:-1]], axis=0)
    whole_out = (timeline[:, :, :width] + carried).transpose(1, 0, 2).reshape(group, blocks * width)
    convolved = lax.all_to_all(whole_out, "seq", split_axis=1, concat_axis=0, tiled=True)
    total = residual.astype(jnp.float32) + out_gate.astype(jnp.float32) * (
        convolved + skip_gain[:, None] * signal_f
    )
    squares = lax.psum(jnp.sum(total * total, axis=0), "ch")
    normed = total * lax.rsqrt(squares / D + 1e-06)[None, :] * norm_gain[:, None]
    return (total.astype(jnp.bfloat16), normed.astype(jnp.bfloat16))


CHUNKS = 2


def spectral_tables(width):
    n = np.arange(width)[:, None]
    k = np.arange(width)[None, :]
    angle = 2.0 * np.pi * (2 * k + 1) * n / (4 * width)
    forward = np.concatenate([np.cos(angle), -np.sin(angle)], axis=1)
    inverse = forward.T / width

    def split(table):
        high = table.astype(jnp.bfloat16)
        low = (table - high.astype(np.float64)).astype(jnp.bfloat16)
        return high, low

    return (
        np.concatenate(split(forward), axis=0),
        np.concatenate(split(inverse), axis=1),
    )


def fused(
    key_hbm, value_hbm, filter_hbm, gate_hbm, residual_hbm, skip_hbm, gain_hbm, forward_hbm, inverse_hbm,
    total_v, scale_ref, columns_v,
    skip_ref, gain_ref, forward_ref, inverse_ref, key_v, value_v, gate_v, residual_v, pair_out, pair_in, spec, joint,
    back_out, back_in, squares_v, load_sem, send_sem, recv_sem, back_send, back_recv, sq_send, sq_recv,
):
    blocks, group, width = key_hbm.shape
    me = lax.axis_index("seq")
    lane = lax.axis_index("ch")
    lanes = squares_v.shape[0]
    rows = group // CHUNKS

    barrier = pltpu.get_barrier_semaphore()
    for step in range(1, lanes):
        pl.semaphore_signal(barrier, inc=1, device_id={"ch": lax.rem(lane + step, lanes)})
    for step in range(1, blocks):
        pl.semaphore_signal(barrier, inc=1, device_id={"seq": lax.rem(me + step, blocks)})
    loads = [
        pltpu.make_async_copy(source, target, load_sem.at[i])
        for i, (source, target) in enumerate(
            ((key_hbm, key_v), (value_hbm, value_v), (filter_hbm, pair_out.at[:, 0]),
             (gate_hbm, gate_v), (residual_hbm, residual_v), (skip_hbm, skip_ref), (gain_hbm, gain_ref),
             (forward_hbm, forward_ref), (inverse_hbm, inverse_ref))
        )
    ]
    for load in loads:
        load.start()
    loads[2].wait()
    loads[0].wait()
    loads[1].wait()
    pair_out[:, 1] = (key_v[...].astype(jnp.float32) * value_v[...].astype(jnp.float32)).astype(jnp.bfloat16)
    pl.semaphore_wait(barrier, blocks - 1 + lanes - 1)

    def outbound(chunk, step):
        peer = lax.rem(me + step, blocks)
        span = pl.ds(chunk * rows, rows)
        return pltpu.make_async_remote_copy(
            src_ref=pair_out.at[peer, :, span],
            dst_ref=pair_in.at[me, :, span],
            send_sem=send_sem.at[chunk, step],
            recv_sem=recv_sem.at[chunk, step],
            device_id={"seq": peer},
        )

    def inbound(chunk, step):
        origin = lax.rem(me + blocks - step, blocks)
        span = pl.ds(chunk * rows, rows)
        return pltpu.make_async_remote_copy(
            src_ref=pair_in.at[origin, :, span],
            dst_ref=pair_in.at[origin, :, span],
            send_sem=send_sem.at[chunk, step],
            recv_sem=recv_sem.at[chunk, step],
            device_id={"seq": origin},
        )

    def returning(chunk, step):
        peer = lax.rem(me + step, blocks)
        span = pl.ds(chunk * rows, rows)
        return pltpu.make_async_remote_copy(
            src_ref=back_out.at[peer, span],
            dst_ref=back_in.at[me, span],
            send_sem=back_send.at[chunk, step],
            recv_sem=back_recv.at[chunk, step],
            device_id={"seq": peer},
        )

    def returned(chunk, step):
        origin = lax.rem(me + blocks - step, blocks)
        span = pl.ds(chunk * rows, rows)
        return pltpu.make_async_remote_copy(
            src_ref=back_in.at[origin, span],
            dst_ref=back_in.at[origin, span],
            send_sem=back_send.at[chunk, step],
            recv_sem=back_recv.at[chunk, step],
            device_id={"seq": origin},
        )

    for chunk in range(CHUNKS):
        for step in range(1, blocks):
            outbound(chunk, step).start()

    pair_in[me] = pair_out[me]
    for load in loads[3:]:
        load.wait()
    for b in range(blocks):
        columns_v[b] = jnp.transpose(jnp.broadcast_to(gain_ref[b : b + 1, :], (width, group)))
        skip = jnp.transpose(jnp.broadcast_to(skip_ref[b : b + 1, :], (width, group)))
        total_v[b] = residual_v[b].astype(jnp.float32) + gate_v[b].astype(jnp.float32) * (
            skip * pair_out[b, 1].astype(jnp.float32)
        )

    sign = (1 - 2 * (lax.broadcasted_iota(jnp.int32, (8, width), 1) % 2)).astype(jnp.float32)

    for chunk in range(CHUNKS):
        for step in range(1, blocks):
            inbound(chunk, step).wait_recv()
        part = pair_in[:, :, chunk * rows : (chunk + 1) * rows, :].reshape(blocks * 2 * rows, width)
        spec[...] = jnp.dot(
            jnp.concatenate([part, part], axis=1), forward_ref[...], preferred_element_type=jnp.float32
        ).reshape(blocks, 2, rows, 2 * width)

        def one_octet(octet, carry):
            span = pl.ds(pl.multiple_of(octet * 8, 8), 8)
            plain_r = [spec[b, 1, span, :width] for b in range(blocks)]
            plain_i = [spec[b, 1, span, width:] for b in range(blocks)]
            input_r, input_i = [plain_r[0]], [plain_i[0]]
            for b in range(1, blocks):
                input_r.append(plain_r[b] - sign * plain_i[b - 1])
                input_i.append(plain_i[b] + sign * plain_r[b - 1])
            taps_r = [spec[b, 0, span, :width] for b in range(blocks)]
            taps_i = [spec[b, 0, span, width:] for b in range(blocks)]
            for j in range(blocks):
                real = taps_r[0] * input_r[j] - taps_i[0] * input_i[j]
                imag = taps_r[0] * input_i[j] + taps_i[0] * input_r[j]
                for d in range(1, j + 1):
                    real = real + taps_r[d] * input_r[j - d] - taps_i[d] * input_i[j - d]
                    imag = imag + taps_r[d] * input_i[j - d] + taps_i[d] * input_r[j - d]
                joint[j, span, :width] = real
                joint[j, span, width:] = imag
            return carry

        lax.fori_loop(0, rows // 8, one_octet, 0)
        timeline = jnp.dot(
            joint[...].reshape(blocks * rows, 2 * width).astype(jnp.bfloat16),
            inverse_ref[...],
            preferred_element_type=jnp.float32,
        )
        timeline = (timeline[:, :width] + timeline[:, width:]).astype(jnp.bfloat16)
        back_out[:, chunk * rows : (chunk + 1) * rows, :] = timeline.reshape(blocks, rows, width)
        for step in range(1, blocks):
            returning(chunk, step).start()
    back_in[me] = back_out[me]

    squares = jnp.zeros((8, width), jnp.float32)
    for chunk in range(CHUNKS):
        for step in range(1, blocks):
            returned(chunk, step).wait_recv()
        for b in range(blocks):
            span = pl.ds(chunk * rows, rows)
            total = total_v[b, span] + gate_v[b, span].astype(jnp.float32) * back_in[b, span].astype(jnp.float32)
            total_v[b, span] = total
            squares = squares + jnp.sum((total * total).reshape(rows // 8, 8, width), axis=0)
    squares_v[lane] = squares

    def share(step, other):
        return pltpu.make_async_remote_copy(
            src_ref=squares_v.at[other[0]],
            dst_ref=squares_v.at[other[0]],
            send_sem=sq_send.at[step],
            recv_sem=sq_recv.at[step],
            device_id={"ch": other[1]},
        )

    for step in range(1, lanes):
        share(step, (lane, lax.rem(lane + step, lanes))).start()
    for step in range(1, lanes):
        origin = lax.rem(lane + lanes - step, lanes)
        share(step, (origin, origin)).wait_recv()
    everyone = jnp.sum(jnp.sum(squares_v[...], axis=0), axis=0, keepdims=True)
    scale_ref[...] = lax.rsqrt(everyone / (lanes * blocks * group) + 1e-06)

    for chunk in range(CHUNKS):
        for step in range(1, blocks):
            outbound(chunk, step).wait_send()
            returning(chunk, step).wait_send()
    for step in range(1, lanes):
        share(step, (lane, lax.rem(lane + step, lanes))).wait_send()


def finish(total_ref, scale_ref, columns_ref, mixed_hbm, normed_hbm, mixed_v, normed_v, mixed_sem, normed_sem):
    blocks = total_ref.shape[0]
    stores = []
    for b in range(blocks):
        mixed_v[b] = total_ref[b].astype(jnp.bfloat16)
        normed_v[b] = (total_ref[b] * scale_ref[...] * columns_ref[b]).astype(jnp.bfloat16)
        stores.append(pltpu.make_async_copy(mixed_v.at[b], mixed_hbm.at[b], mixed_sem.at[b]))
        stores.append(pltpu.make_async_copy(normed_v.at[b], normed_hbm.at[b], normed_sem.at[b]))
        stores[-2].start()
        stores[-1].start()
    for store in stores:
        store.wait()


def with_kernel(out_gate, key_proj, value_proj, long_filter, skip_gain, residual, norm_gain):
    chans, width = key_proj.shape
    blocks, lanes = lax.axis_size("seq"), lax.axis_size("ch")
    group = chans // blocks
    rows = group // CHUNKS
    shape = (blocks, group, width)
    forward, inverse = spectral_tables(width)
    bf16, f32 = jnp.bfloat16, jnp.float32
    anywhere = pl.BlockSpec(memory_space=pl.ANY)
    local = pl.BlockSpec(memory_space=pltpu.VMEM)
    dma = pltpu.SemaphoreType.DMA
    total, scale, columns = pl.pallas_call(
        fused,
        out_shape=(pltpu.VMEM(shape, f32), pltpu.VMEM((1, width), f32), pltpu.VMEM(shape, f32)),
        in_specs=[anywhere] * 9,
        out_specs=(local, local, local),
        scratch_shapes=[
            pltpu.VMEM((blocks, group), f32),
            pltpu.VMEM((blocks, group), f32),
            pltpu.VMEM((2 * width, 2 * width), bf16),
            pltpu.VMEM((2 * width, 2 * width), bf16),
            *[pltpu.VMEM(shape, bf16) for _ in range(4)],
            *[pltpu.VMEM((blocks, 2, group, width), bf16) for _ in range(2)],
            pltpu.VMEM((blocks, 2, rows, 2 * width), f32),
            pltpu.VMEM((blocks, rows, 2 * width), f32),
            pltpu.VMEM(shape, bf16),
            pltpu.VMEM(shape, bf16),
            pltpu.VMEM((lanes, 8, width), f32),
            dma((9,)),
            dma((CHUNKS, blocks)),
            dma((CHUNKS, blocks)),
            dma((CHUNKS, blocks)),
            dma((CHUNKS, blocks)),
            dma((lanes,)),
            dma((lanes,)),
        ],
        compiler_params=pltpu.CompilerParams(collective_id=0, has_side_effects=True),
    )(
        key_proj.reshape(shape),
        value_proj.reshape(shape),
        long_filter.reshape(shape),
        out_gate.reshape(shape),
        residual.reshape(shape),
        skip_gain.reshape(blocks, group),
        norm_gain.reshape(blocks, group),
        jnp.asarray(forward),
        jnp.asarray(inverse),
    )
    mixed, normed = pl.pallas_call(
        finish,
        out_shape=(jax.ShapeDtypeStruct(shape, bf16), jax.ShapeDtypeStruct(shape, bf16)),
        in_specs=[local, local, local],
        out_specs=(anywhere, anywhere),
        scratch_shapes=[
            pltpu.VMEM(shape, bf16),
            pltpu.VMEM(shape, bf16),
            dma((blocks,)),
            dma((blocks,)),
        ],
    )(
        pltpu.with_memory_space_constraint(total, pltpu.VMEM),
        pltpu.with_memory_space_constraint(scale, pltpu.VMEM),
        pltpu.with_memory_space_constraint(columns, pltpu.VMEM),
    )
    return mixed.reshape(chans, width), normed.reshape(chans, width)


def choose(out_gate, key_proj, *rest):
    chans, width = key_proj.shape
    blocks = lax.axis_size("seq")
    tiled = chans % (blocks * CHUNKS * 16) == 0 and width % 128 == 0 and blocks <= 16
    return (with_kernel if tiled else on_device)(out_gate, key_proj, *rest)


def solution(mesh):
    return jax.shard_map(
        choose,
        mesh=mesh,
        in_specs=(
            P("ch", "seq"),
            P("ch", "seq"),
            P("ch", "seq"),
            P("ch", "seq"),
            P("ch"),
            P("ch", "seq"),
            P("ch"),
        ),
        out_specs=(P("ch", "seq"), P("ch", "seq")),
        check_vma=False,
    )
```

```python
import math

import numpy as np

import jax
import jax.numpy as jnp
from jax import lax
from jax.experimental import pallas as pl
from jax.experimental.pallas import tpu as pltpu
from jax.sharding import PartitionSpec as P

D = 4096


HIGHEST = lax.Precision.HIGHEST


def tables(count, span, period):
    row_ids = jnp.arange(count, dtype=jnp.int32)[:, None]
    col_ids = jnp.arange(span, dtype=jnp.int32)[None, :]
    phases = (row_ids * col_ids % period).astype(jnp.float32) * (2.0 * math.pi / period)
    return (jnp.cos(phases), jnp.sin(phases))


def product(left, right):
    return jnp.dot(left, right, precision=HIGHEST, preferred_element_type=jnp.float32)


def block_spectrum(signal):
    width = signal.shape[1]
    cosine, sine = tables(width, 2 * width, 2 * width)
    return (product(signal, cosine), -product(signal, sine))


def block_inverse(real_part, imag_part):
    span = real_part.shape[1]
    cosine, sine = tables(span, span, span)
    return (product(real_part, cosine) - product(imag_part, sine)) / span


def index_convolve(input_real, input_imag, filter_real, filter_imag):
    blocks = input_real.shape[0]
    forward_cos, forward_sin = tables(2 * blocks, blocks, 2 * blocks)

    def forward(real_part, imag_part):
        return (
            product(forward_cos, real_part) + product(forward_sin, imag_part),
            product(forward_cos, imag_part) - product(forward_sin, real_part),
        )

    signal_real, signal_imag = forward(input_real, input_imag)
    kernel_real, kernel_imag = forward(filter_real, filter_imag)
    joint_real = signal_real * kernel_real - signal_imag * kernel_imag
    joint_imag = signal_real * kernel_imag + signal_imag * kernel_real
    back_cos, back_sin = tables(blocks, 2 * blocks, 2 * blocks)
    result_real = (product(back_cos, joint_real) - product(back_sin, joint_imag)) / (2 * blocks)
    result_imag = (product(back_cos, joint_imag) + product(back_sin, joint_real)) / (2 * blocks)
    return (result_real, result_imag)


def on_device(out_gate, key_proj, value_proj, long_filter, skip_gain, residual, norm_gain):
    chans, width = key_proj.shape
    blocks = lax.axis_size("seq")
    product_in = (key_proj.astype(jnp.float32) * value_proj.astype(jnp.float32)).astype(
        jnp.bfloat16
    )
    signal_f = product_in.astype(jnp.float32)
    whole_in, whole_filter = (
        lax.all_to_all(product_in, "seq", split_axis=0, concat_axis=1, tiled=True),
        lax.all_to_all(long_filter, "seq", split_axis=0, concat_axis=1, tiled=True),
    )
    group = whole_in.shape[0]

    def by_block(array):
        return (
            array.astype(jnp.float32)
            .reshape(group, blocks, width)
            .transpose(1, 0, 2)
            .reshape(blocks * group, width)
        )

    signal_real, signal_imag = block_spectrum(by_block(whole_in))
    kernel_real, kernel_imag = block_spectrum(by_block(whole_filter))
    result_real, result_imag = index_convolve(
        signal_real.reshape(blocks, -1),
        signal_imag.reshape(blocks, -1),
        kernel_real.reshape(blocks, -1),
        kernel_imag.reshape(blocks, -1),
    )
    timeline = block_inverse(
        result_real.reshape(blocks * group, 2 * width),
        result_imag.reshape(blocks * group, 2 * width),
    ).reshape(blocks, group, 2 * width)
    upper = timeline[:, :, width:]
    carried = jnp.concatenate([jnp.zeros((1, group, width), jnp.float32), upper[:-1]], axis=0)
    whole_out = (timeline[:, :, :width] + carried).transpose(1, 0, 2).reshape(group, blocks * width)
    convolved = lax.all_to_all(whole_out, "seq", split_axis=1, concat_axis=0, tiled=True)
    total = residual.astype(jnp.float32) + out_gate.astype(jnp.float32) * (
        convolved + skip_gain[:, None] * signal_f
    )
    squares = lax.psum(jnp.sum(total * total, axis=0), "ch")
    normed = total * lax.rsqrt(squares / D + 1e-06)[None, :] * norm_gain[:, None]
    return (total.astype(jnp.bfloat16), normed.astype(jnp.bfloat16))


PARTS = (5, 3)
CHUNKS = len(PARTS)
WHOLE = sum(PARTS)


def spectral_tables(width):
    n = np.arange(width)[:, None]
    k = np.arange(width)[None, :]
    angle = 2.0 * np.pi * (2 * k + 1) * n / (4 * width)
    forward = np.concatenate([np.cos(angle), -np.sin(angle)], axis=1)
    inverse = forward.T / width

    def split(table):
        high = table.astype(jnp.bfloat16)
        low = (table - high.astype(np.float64)).astype(jnp.bfloat16)
        return high, low

    return (
        np.concatenate(split(forward), axis=0),
        np.concatenate(split(inverse), axis=1),
    )


def fused(
    key_hbm, value_hbm, filter_hbm, gate_hbm, residual_hbm, skip_hbm, gain_hbm, forward_hbm, inverse_hbm,
    total_v, scale_ref, columns_v,
    skip_ref, gain_ref, forward_ref, inverse_ref, key_v, value_v, gate_v, residual_v, pair_out, pair_in, spec, joint,
    back_out, back_in, squares_v, load_sem, send_sem, recv_sem, back_send, back_recv, sq_send, sq_recv,
):
    blocks, group, width = key_hbm.shape
    me = lax.axis_index("seq")
    lane = lax.axis_index("ch")
    lanes = squares_v.shape[0]
    heights = [group * part // WHOLE for part in PARTS]
    firsts = [sum(heights[:i]) for i in range(CHUNKS)]

    barrier = pltpu.get_barrier_semaphore()
    for step in range(1, lanes):
        pl.semaphore_signal(barrier, inc=1, device_id={"ch": lax.rem(lane + step, lanes)})
    for step in range(1, blocks):
        pl.semaphore_signal(barrier, inc=1, device_id={"seq": lax.rem(me + step, blocks)})
    loads = [
        pltpu.make_async_copy(source, target, load_sem.at[i])
        for i, (source, target) in enumerate(
            ((key_hbm, key_v), (value_hbm, value_v), (filter_hbm, pair_out.at[:, 0]),
             (gate_hbm, gate_v), (residual_hbm, residual_v), (skip_hbm, skip_ref), (gain_hbm, gain_ref),
             (forward_hbm, forward_ref), (inverse_hbm, inverse_ref))
        )
    ]
    for load in loads:
        load.start()
    loads[2].wait()
    loads[0].wait()
    loads[1].wait()
    pair_out[:, 1] = (key_v[...].astype(jnp.float32) * value_v[...].astype(jnp.float32)).astype(jnp.bfloat16)
    pl.semaphore_wait(barrier, blocks - 1 + lanes - 1)

    def partner(step):
        peer, bit = me, 1
        while bit <= step:
            if step & bit:
                peer = peer + bit - 2 * bit * lax.rem(me // bit, 2)
            bit *= 2
        return peer

    order = sorted(range(1, blocks), key=lambda step: (-(step // 2).bit_count(), -step))

    def outbound(chunk, step):
        peer = partner(step)
        span = pl.ds(firsts[chunk], heights[chunk])
        return pltpu.make_async_remote_copy(
            src_ref=pair_out.at[peer, :, span],
            dst_ref=pair_in.at[me, :, span],
            send_sem=send_sem.at[chunk, step],
            recv_sem=recv_sem.at[chunk, step],
            device_id={"seq": peer},
        )

    def inbound(chunk, step):
        origin = partner(step)
        span = pl.ds(firsts[chunk], heights[chunk])
        return pltpu.make_async_remote_copy(
            src_ref=pair_in.at[origin, :, span],
            dst_ref=pair_in.at[origin, :, span],
            send_sem=send_sem.at[chunk, step],
            recv_sem=recv_sem.at[chunk, step],
            device_id={"seq": origin},
        )

    def returning(chunk, step):
        peer = partner(step)
        span = pl.ds(firsts[chunk], heights[chunk])
        return pltpu.make_async_remote_copy(
            src_ref=back_out.at[peer, span],
            dst_ref=back_in.at[me, span],
            send_sem=back_send.at[chunk, step],
            recv_sem=back_recv.at[chunk, step],
            device_id={"seq": peer},
        )

    def returned(chunk, step):
        origin = partner(step)
        span = pl.ds(firsts[chunk], heights[chunk])
        return pltpu.make_async_remote_copy(
            src_ref=back_in.at[origin, span],
            dst_ref=back_in.at[origin, span],
            send_sem=back_send.at[chunk, step],
            recv_sem=back_recv.at[chunk, step],
            device_id={"seq": origin},
        )

    for chunk in range(CHUNKS):
        for step in order:
            outbound(chunk, step).start()

    pair_in[me] = pair_out[me]
    for load in loads[3:]:
        load.wait()
    for b in range(blocks):
        columns_v[b] = jnp.transpose(jnp.broadcast_to(gain_ref[b : b + 1, :], (width, group)))
        skip = jnp.transpose(jnp.broadcast_to(skip_ref[b : b + 1, :], (width, group)))
        total_v[b] = residual_v[b].astype(jnp.float32) + gate_v[b].astype(jnp.float32) * (
            skip * pair_out[b, 1].astype(jnp.float32)
        )

    sign = (1 - 2 * (lax.broadcasted_iota(jnp.int32, (8, width), 1) % 2)).astype(jnp.float32)

    for chunk in range(CHUNKS):
        first, rows = firsts[chunk], heights[chunk]
        for step in order:
            inbound(chunk, step).wait_recv()
        part = pair_in[:, :, first : first + rows, :].reshape(blocks * 2 * rows, width)
        spec[:, :, :rows] = jnp.dot(
            jnp.concatenate([part, part], axis=1), forward_ref[...], preferred_element_type=jnp.float32
        ).reshape(blocks, 2, rows, 2 * width)

        def one_octet(octet, carry):
            span = pl.ds(pl.multiple_of(octet * 8, 8), 8)
            plain_r = [spec[b, 1, span, :width] for b in range(blocks)]
            plain_i = [spec[b, 1, span, width:] for b in range(blocks)]
            input_r, input_i = [plain_r[0]], [plain_i[0]]
            for b in range(1, blocks):
                input_r.append(plain_r[b] - sign * plain_i[b - 1])
                input_i.append(plain_i[b] + sign * plain_r[b - 1])
            taps_r = [spec[b, 0, span, :width] for b in range(blocks)]
            taps_i = [spec[b, 0, span, width:] for b in range(blocks)]
            for j in range(blocks):
                real = taps_r[0] * input_r[j] - taps_i[0] * input_i[j]
                imag = taps_r[0] * input_i[j] + taps_i[0] * input_r[j]
                for d in range(1, j + 1):
                    real = real + taps_r[d] * input_r[j - d] - taps_i[d] * input_i[j - d]
                    imag = imag + taps_r[d] * input_i[j - d] + taps_i[d] * input_r[j - d]
                joint[j, span, :width] = real
                joint[j, span, width:] = imag
            return carry

        lax.fori_loop(0, rows // 8, one_octet, 0)
        timeline = jnp.dot(
            joint[:, :rows].reshape(blocks * rows, 2 * width).astype(jnp.bfloat16),
            inverse_ref[...],
            preferred_element_type=jnp.float32,
        )
        timeline = (timeline[:, :width] + timeline[:, width:]).astype(jnp.bfloat16)
        back_out[:, first : first + rows, :] = timeline.reshape(blocks, rows, width)
        for step in order:
            returning(chunk, step).start()
    back_in[me] = back_out[me]

    squares = jnp.zeros((8, width), jnp.float32)
    for chunk in range(CHUNKS):
        for step in [0] + order[::-1]:
            if step:
                returned(chunk, step).wait_recv()
            b = partner(step)
            span = pl.ds(firsts[chunk], heights[chunk])
            total = total_v[b, span] + gate_v[b, span].astype(jnp.float32) * back_in[b, span].astype(jnp.float32)
            total_v[b, span] = total
            squares = squares + jnp.sum((total * total).reshape(heights[chunk] // 8, 8, width), axis=0)
    squares_v[lane] = jnp.sum(squares, axis=0, keepdims=True)

    def share(step, other):
        return pltpu.make_async_remote_copy(
            src_ref=squares_v.at[other[0]],
            dst_ref=squares_v.at[other[0]],
            send_sem=sq_send.at[step],
            recv_sem=sq_recv.at[step],
            device_id={"ch": other[1]},
        )

    for step in range(1, lanes):
        share(step, (lane, lax.rem(lane + step, lanes))).start()
    for step in range(1, lanes):
        origin = lax.rem(lane + lanes - step, lanes)
        share(step, (origin, origin)).wait_recv()
    everyone = jnp.sum(squares_v[...], axis=0)
    scale_ref[...] = lax.rsqrt(everyone / (lanes * blocks * group) + 1e-06)

    for chunk in range(CHUNKS):
        for step in order:
            outbound(chunk, step).wait_send()
            returning(chunk, step).wait_send()
    for step in range(1, lanes):
        share(step, (lane, lax.rem(lane + step, lanes))).wait_send()


def finish(total_ref, scale_ref, columns_ref, mixed_hbm, normed_hbm, mixed_v, normed_v, mixed_sem, normed_sem):
    blocks = total_ref.shape[0]
    stores = []
    for b in range(blocks):
        mixed_v[b] = total_ref[b].astype(jnp.bfloat16)
        normed_v[b] = (total_ref[b] * scale_ref[...] * columns_ref[b]).astype(jnp.bfloat16)
        stores.append(pltpu.make_async_copy(mixed_v.at[b], mixed_hbm.at[b], mixed_sem.at[b]))
        stores.append(pltpu.make_async_copy(normed_v.at[b], normed_hbm.at[b], normed_sem.at[b]))
        stores[-2].start()
        stores[-1].start()
    for store in stores:
        store.wait()


def with_kernel(out_gate, key_proj, value_proj, long_filter, skip_gain, residual, norm_gain):
    chans, width = key_proj.shape
    blocks, lanes = lax.axis_size("seq"), lax.axis_size("ch")
    group = chans // blocks
    rows = group * max(PARTS) // WHOLE
    shape = (blocks, group, width)
    forward, inverse = spectral_tables(width)
    bf16, f32 = jnp.bfloat16, jnp.float32
    anywhere = pl.BlockSpec(memory_space=pl.ANY)
    local = pl.BlockSpec(memory_space=pltpu.VMEM)
    dma = pltpu.SemaphoreType.DMA
    total, scale, columns = pl.pallas_call(
        fused,
        out_shape=(pltpu.VMEM(shape, f32), pltpu.VMEM((1, width), f32), pltpu.VMEM(shape, f32)),
        in_specs=[anywhere] * 9,
        out_specs=(local, local, local),
        scratch_shapes=[
            pltpu.VMEM((blocks, group), f32),
            pltpu.VMEM((blocks, group), f32),
            pltpu.VMEM((2 * width, 2 * width), bf16),
            pltpu.VMEM((2 * width, 2 * width), bf16),
            *[pltpu.VMEM(shape, bf16) for _ in range(4)],
            *[pltpu.VMEM((blocks, 2, group, width), bf16) for _ in range(2)],
            pltpu.VMEM((blocks, 2, rows, 2 * width), f32),
            pltpu.VMEM((blocks, rows, 2 * width), f32),
            pltpu.VMEM(shape, bf16),
            pltpu.VMEM(shape, bf16),
            pltpu.VMEM((lanes, 1, width), f32),
            dma((9,)),
            dma((CHUNKS, blocks)),
            dma((CHUNKS, blocks)),
            dma((CHUNKS, blocks)),
            dma((CHUNKS, blocks)),
            dma((lanes,)),
            dma((lanes,)),
        ],
        compiler_params=pltpu.CompilerParams(collective_id=0, has_side_effects=True),
    )(
        key_proj.reshape(shape),
        value_proj.reshape(shape),
        long_filter.reshape(shape),
        out_gate.reshape(shape),
        residual.reshape(shape),
        skip_gain.reshape(blocks, group),
        norm_gain.reshape(blocks, group),
        jnp.asarray(forward),
        jnp.asarray(inverse),
    )
    mixed, normed = pl.pallas_call(
        finish,
        out_shape=(jax.ShapeDtypeStruct(shape, bf16), jax.ShapeDtypeStruct(shape, bf16)),
        in_specs=[local, local, local],
        out_specs=(anywhere, anywhere),
        scratch_shapes=[
            pltpu.VMEM(shape, bf16),
            pltpu.VMEM(shape, bf16),
            dma((blocks,)),
            dma((blocks,)),
        ],
    )(
        pltpu.with_memory_space_constraint(total, pltpu.VMEM),
        pltpu.with_memory_space_constraint(scale, pltpu.VMEM),
        pltpu.with_memory_space_constraint(columns, pltpu.VMEM),
    )
    return mixed.reshape(chans, width), normed.reshape(chans, width)


def choose(out_gate, key_proj, *rest):
    chans, width = key_proj.shape
    blocks = lax.axis_size("seq")
    tiled = blocks & (blocks - 1) == 0 and chans % (blocks * WHOLE * 16) == 0 and width % 128 == 0 and blocks <= 16
    return (with_kernel if tiled else on_device)(out_gate, key_proj, *rest)


def solution(mesh):
    return jax.shard_map(
        choose,
        mesh=mesh,
        in_specs=(
            P("ch", "seq"),
            P("ch", "seq"),
            P("ch", "seq"),
            P("ch", "seq"),
            P("ch"),
            P("ch", "seq"),
            P("ch"),
        ),
        out_specs=(P("ch", "seq"), P("ch", "seq")),
        check_vma=False,
    )
```

```python
import math

import numpy as np

import jax
import jax.numpy as jnp
from jax import lax
from jax.experimental import pallas as pl
from jax.experimental.pallas import tpu as pltpu
from jax.sharding import PartitionSpec as P

D = 4096


HIGHEST = lax.Precision.HIGHEST


def tables(count, span, period):
    row_ids = jnp.arange(count, dtype=jnp.int32)[:, None]
    col_ids = jnp.arange(span, dtype=jnp.int32)[None, :]
    phases = (row_ids * col_ids % period).astype(jnp.float32) * (2.0 * math.pi / period)
    return (jnp.cos(phases), jnp.sin(phases))


def product(left, right):
    return jnp.dot(left, right, precision=HIGHEST, preferred_element_type=jnp.float32)


def block_spectrum(signal):
    width = signal.shape[1]
    cosine, sine = tables(width, 2 * width, 2 * width)
    return (product(signal, cosine), -product(signal, sine))


def block_inverse(real_part, imag_part):
    span = real_part.shape[1]
    cosine, sine = tables(span, span, span)
    return (product(real_part, cosine) - product(imag_part, sine)) / span


def index_convolve(input_real, input_imag, filter_real, filter_imag):
    blocks = input_real.shape[0]
    forward_cos, forward_sin = tables(2 * blocks, blocks, 2 * blocks)

    def forward(real_part, imag_part):
        return (
            product(forward_cos, real_part) + product(forward_sin, imag_part),
            product(forward_cos, imag_part) - product(forward_sin, real_part),
        )

    signal_real, signal_imag = forward(input_real, input_imag)
    kernel_real, kernel_imag = forward(filter_real, filter_imag)
    joint_real = signal_real * kernel_real - signal_imag * kernel_imag
    joint_imag = signal_real * kernel_imag + signal_imag * kernel_real
    back_cos, back_sin = tables(blocks, 2 * blocks, 2 * blocks)
    result_real = (product(back_cos, joint_real) - product(back_sin, joint_imag)) / (2 * blocks)
    result_imag = (product(back_cos, joint_imag) + product(back_sin, joint_real)) / (2 * blocks)
    return (result_real, result_imag)


def on_device(out_gate, key_proj, value_proj, long_filter, skip_gain, residual, norm_gain):
    chans, width = key_proj.shape
    blocks = lax.axis_size("seq")
    product_in = (key_proj.astype(jnp.float32) * value_proj.astype(jnp.float32)).astype(
        jnp.bfloat16
    )
    signal_f = product_in.astype(jnp.float32)
    whole_in, whole_filter = (
        lax.all_to_all(product_in, "seq", split_axis=0, concat_axis=1, tiled=True),
        lax.all_to_all(long_filter, "seq", split_axis=0, concat_axis=1, tiled=True),
    )
    group = whole_in.shape[0]

    def by_block(array):
        return (
            array.astype(jnp.float32)
            .reshape(group, blocks, width)
            .transpose(1, 0, 2)
            .reshape(blocks * group, width)
        )

    signal_real, signal_imag = block_spectrum(by_block(whole_in))
    kernel_real, kernel_imag = block_spectrum(by_block(whole_filter))
    result_real, result_imag = index_convolve(
        signal_real.reshape(blocks, -1),
        signal_imag.reshape(blocks, -1),
        kernel_real.reshape(blocks, -1),
        kernel_imag.reshape(blocks, -1),
    )
    timeline = block_inverse(
        result_real.reshape(blocks * group, 2 * width),
        result_imag.reshape(blocks * group, 2 * width),
    ).reshape(blocks, group, 2 * width)
    upper = timeline[:, :, width:]
    carried = jnp.concatenate([jnp.zeros((1, group, width), jnp.float32), upper[:-1]], axis=0)
    whole_out = (timeline[:, :, :width] + carried).transpose(1, 0, 2).reshape(group, blocks * width)
    convolved = lax.all_to_all(whole_out, "seq", split_axis=1, concat_axis=0, tiled=True)
    total = residual.astype(jnp.float32) + out_gate.astype(jnp.float32) * (
        convolved + skip_gain[:, None] * signal_f
    )
    squares = lax.psum(jnp.sum(total * total, axis=0), "ch")
    normed = total * lax.rsqrt(squares / D + 1e-06)[None, :] * norm_gain[:, None]
    return (total.astype(jnp.bfloat16), normed.astype(jnp.bfloat16))


PARTS = (5, 3)
CHUNKS = len(PARTS)
WHOLE = sum(PARTS)


def spectral_tables(width):
    n = np.arange(width)[:, None]
    k = np.arange(width)[None, :]
    angle = 2.0 * np.pi * (2 * k + 1) * n / (4 * width)
    forward = np.concatenate([np.cos(angle), -np.sin(angle)], axis=1)
    inverse = forward.T / width

    def split(table):
        high = table.astype(jnp.bfloat16)
        low = (table - high.astype(np.float64)).astype(jnp.bfloat16)
        return high, low

    return (
        np.concatenate(split(forward), axis=0),
        np.concatenate(split(inverse), axis=1),
    )


def fused(
    key_hbm, value_hbm, filter_hbm, gate_hbm, residual_hbm, skip_hbm, gain_hbm, forward_hbm, inverse_hbm,
    total_v, scale_ref, columns_v,
    skip_ref, gain_ref, forward_ref, inverse_ref, key_v, value_v, gate_v, residual_v, pair_out, pair_in, spec, joint,
    back_out, back_in, squares_v, load_sem, send_sem, recv_sem, back_send, back_recv, sq_send, sq_recv,
):
    blocks, group, width = key_hbm.shape
    me = lax.axis_index("seq")
    lane = lax.axis_index("ch")
    lanes = squares_v.shape[0]
    heights = [group * part // WHOLE for part in PARTS]
    firsts = [sum(heights[:i]) for i in range(CHUNKS)]

    barrier = pltpu.get_barrier_semaphore()
    for step in range(1, lanes):
        pl.semaphore_signal(barrier, inc=1, device_id={"ch": lax.rem(lane + step, lanes)})
    for step in range(1, blocks):
        pl.semaphore_signal(barrier, inc=1, device_id={"seq": lax.rem(me + step, blocks)})
    loads = [
        pltpu.make_async_copy(source, target, load_sem.at[i])
        for i, (source, target) in enumerate(
            ((key_hbm, key_v), (value_hbm, value_v), (filter_hbm, pair_out.at[:, 0]),
             (gate_hbm, gate_v), (residual_hbm, residual_v), (skip_hbm, skip_ref), (gain_hbm, gain_ref),
             (forward_hbm, forward_ref), (inverse_hbm, inverse_ref))
        )
    ]
    for load in loads:
        load.start()
    loads[2].wait()
    loads[0].wait()
    loads[1].wait()
    pair_out[:, 1] = (key_v[...].astype(jnp.float32) * value_v[...].astype(jnp.float32)).astype(jnp.bfloat16)
    pl.semaphore_wait(barrier, blocks - 1 + lanes - 1)

    def partner(step):
        peer, bit = me, 1
        while bit <= step:
            if step & bit:
                peer = peer + bit - 2 * bit * lax.rem(me // bit, 2)
            bit *= 2
        return peer

    order = sorted(range(1, blocks), key=lambda step: (-(step // 2).bit_count(), -step))

    def outbound(chunk, step):
        peer = partner(step)
        span = pl.ds(firsts[chunk], heights[chunk])
        return pltpu.make_async_remote_copy(
            src_ref=pair_out.at[peer, :, span],
            dst_ref=pair_in.at[me, :, span],
            send_sem=send_sem.at[chunk, step],
            recv_sem=recv_sem.at[chunk, step],
            device_id={"seq": peer},
        )

    def inbound(chunk, step):
        origin = partner(step)
        span = pl.ds(firsts[chunk], heights[chunk])
        return pltpu.make_async_remote_copy(
            src_ref=pair_in.at[origin, :, span],
            dst_ref=pair_in.at[origin, :, span],
            send_sem=send_sem.at[chunk, step],
            recv_sem=recv_sem.at[chunk, step],
            device_id={"seq": origin},
        )

    def returning(chunk, step):
        peer = partner(step)
        span = pl.ds(firsts[chunk], heights[chunk])
        return pltpu.make_async_remote_copy(
            src_ref=back_out.at[peer, span],
            dst_ref=back_in.at[me, span],
            send_sem=back_send.at[chunk, step],
            recv_sem=back_recv.at[chunk, step],
            device_id={"seq": peer},
        )

    def returned(chunk, step):
        origin = partner(step)
        span = pl.ds(firsts[chunk], heights[chunk])
        return pltpu.make_async_remote_copy(
            src_ref=back_in.at[origin, span],
            dst_ref=back_in.at[origin, span],
            send_sem=back_send.at[chunk, step],
            recv_sem=back_recv.at[chunk, step],
            device_id={"seq": origin},
        )

    for chunk in range(CHUNKS):
        for step in order:
            outbound(chunk, step).start()

    pair_in[me] = pair_out[me]
    for load in loads[3:]:
        load.wait()
    for b in range(blocks):
        columns_v[b] = jnp.transpose(jnp.broadcast_to(gain_ref[b : b + 1, :], (width, group)))
        skip = jnp.transpose(jnp.broadcast_to(skip_ref[b : b + 1, :], (width, group)))
        total_v[b] = residual_v[b].astype(jnp.float32) + gate_v[b].astype(jnp.float32) * (
            skip * pair_out[b, 1].astype(jnp.float32)
        )

    sign = (1 - 2 * (lax.broadcasted_iota(jnp.int32, (8, width), 1) % 2)).astype(jnp.float32)

    for chunk in range(CHUNKS):
        first, rows = firsts[chunk], heights[chunk]
        for step in order:
            inbound(chunk, step).wait_recv()
        part = pair_in[:, :, first : first + rows, :].reshape(blocks * 2 * rows, width)
        spec[:, :, :rows] = jnp.dot(
            jnp.concatenate([part, part], axis=1), forward_ref[...], preferred_element_type=jnp.float32
        ).reshape(blocks, 2, rows, 2 * width)

        def one_octet(octet, carry):
            span = pl.ds(pl.multiple_of(octet * 8, 8), 8)
            plain_r = [spec[b, 1, span, :width] for b in range(blocks)]
            plain_i = [spec[b, 1, span, width:] for b in range(blocks)]
            input_r, input_i = [plain_r[0]], [plain_i[0]]
            for b in range(1, blocks):
                input_r.append(plain_r[b] - sign * plain_i[b - 1])
                input_i.append(plain_i[b] + sign * plain_r[b - 1])
            taps_r = [spec[b, 0, span, :width] for b in range(blocks)]
            taps_i = [spec[b, 0, span, width:] for b in range(blocks)]
            for j in range(blocks):
                real = taps_r[0] * input_r[j] - taps_i[0] * input_i[j]
                imag = taps_r[0] * input_i[j] + taps_i[0] * input_r[j]
                for d in range(1, j + 1):
                    real = real + taps_r[d] * input_r[j - d] - taps_i[d] * input_i[j - d]
                    imag = imag + taps_r[d] * input_i[j - d] + taps_i[d] * input_r[j - d]
                joint[j, span, :width] = real
                joint[j, span, width:] = imag
            return carry

        lax.fori_loop(0, rows // 8, one_octet, 0)
        timeline = jnp.dot(
            joint[:, :rows].reshape(blocks * rows, 2 * width).astype(jnp.bfloat16),
            inverse_ref[...],
            preferred_element_type=jnp.float32,
        )
        timeline = (timeline[:, :width] + timeline[:, width:]).astype(jnp.bfloat16)
        back_out[:, first : first + rows, :] = timeline.reshape(blocks, rows, width)
        for step in order:
            returning(chunk, step).start()
    back_in[me] = back_out[me]

    squares = jnp.zeros((8, width), jnp.float32)
    for chunk in range(CHUNKS):
        for step in [0] + order[::-1]:
            if step:
                returned(chunk, step).wait_recv()
            b = partner(step)
            span = pl.ds(firsts[chunk], heights[chunk])
            total = total_v[b, span] + gate_v[b, span].astype(jnp.float32) * back_in[b, span].astype(jnp.float32)
            total_v[b, span] = total
            squares = squares + jnp.sum((total * total).reshape(heights[chunk] // 8, 8, width), axis=0)
    squares_v[lane] = jnp.sum(squares, axis=0, keepdims=True)

    def share(step, other):
        return pltpu.make_async_remote_copy(
            src_ref=squares_v.at[other[0]],
            dst_ref=squares_v.at[other[0]],
            send_sem=sq_send.at[step],
            recv_sem=sq_recv.at[step],
            device_id={"ch": other[1]},
        )

    for step in range(1, lanes):
        share(step, (lane, lax.rem(lane + step, lanes))).start()
    for step in range(1, lanes):
        origin = lax.rem(lane + lanes - step, lanes)
        share(step, (origin, origin)).wait_recv()
    everyone = jnp.sum(squares_v[...], axis=0)
    scale_ref[...] = lax.rsqrt(everyone / (lanes * blocks * group) + 1e-06)

    for chunk in range(CHUNKS):
        for step in order:
            outbound(chunk, step).wait_send()
            returning(chunk, step).wait_send()
    for step in range(1, lanes):
        share(step, (lane, lax.rem(lane + step, lanes))).wait_send()


def finish(total_ref, scale_ref, columns_ref, mixed_hbm, normed_hbm, mixed_v, normed_v, mixed_sem, normed_sem):
    blocks = total_ref.shape[0]
    stores = []
    half = blocks // 2
    for b in range(blocks):
        mixed_v[b] = total_ref[b].astype(jnp.bfloat16)
        normed_v[b] = (total_ref[b] * scale_ref[...] * columns_ref[b]).astype(jnp.bfloat16)
        if (b + 1) % half == 0:
            part = pl.ds(b + 1 - half, half)
            stores.append(pltpu.make_async_copy(mixed_v.at[part], mixed_hbm.at[part], mixed_sem.at[b]))
            stores.append(pltpu.make_async_copy(normed_v.at[part], normed_hbm.at[part], normed_sem.at[b]))
            stores[-2].start()
            stores[-1].start()
    for store in stores:
        store.wait()


def with_kernel(out_gate, key_proj, value_proj, long_filter, skip_gain, residual, norm_gain):
    chans, width = key_proj.shape
    blocks, lanes = lax.axis_size("seq"), lax.axis_size("ch")
    group = chans // blocks
    rows = group * max(PARTS) // WHOLE
    shape = (blocks, group, width)
    forward, inverse = spectral_tables(width)
    bf16, f32 = jnp.bfloat16, jnp.float32
    anywhere = pl.BlockSpec(memory_space=pl.ANY)
    local = pl.BlockSpec(memory_space=pltpu.VMEM)
    dma = pltpu.SemaphoreType.DMA
    total, scale, columns = pl.pallas_call(
        fused,
        out_shape=(pltpu.VMEM(shape, f32), pltpu.VMEM((1, width), f32), pltpu.VMEM(shape, f32)),
        in_specs=[anywhere] * 9,
        out_specs=(local, local, local),
        scratch_shapes=[
            pltpu.VMEM((blocks, group), f32),
            pltpu.VMEM((blocks, group), f32),
            pltpu.VMEM((2 * width, 2 * width), bf16),
            pltpu.VMEM((2 * width, 2 * width), bf16),
            *[pltpu.VMEM(shape, bf16) for _ in range(4)],
            *[pltpu.VMEM((blocks, 2, group, width), bf16) for _ in range(2)],
            pltpu.VMEM((blocks, 2, rows, 2 * width), f32),
            pltpu.VMEM((blocks, rows, 2 * width), f32),
            pltpu.VMEM(shape, bf16),
            pltpu.VMEM(shape, bf16),
            pltpu.VMEM((lanes, 1, width), f32),
            dma((9,)),
            dma((CHUNKS, blocks)),
            dma((CHUNKS, blocks)),
            dma((CHUNKS, blocks)),
            dma((CHUNKS, blocks)),
            dma((lanes,)),
            dma((lanes,)),
        ],
        compiler_params=pltpu.CompilerParams(collective_id=0, has_side_effects=True),
    )(
        key_proj.reshape(shape),
        value_proj.reshape(shape),
        long_filter.reshape(shape),
        out_gate.reshape(shape),
        residual.reshape(shape),
        skip_gain.reshape(blocks, group),
        norm_gain.reshape(blocks, group),
        jnp.asarray(forward),
        jnp.asarray(inverse),
    )
    mixed, normed = pl.pallas_call(
        finish,
        out_shape=(jax.ShapeDtypeStruct(shape, bf16), jax.ShapeDtypeStruct(shape, bf16)),
        in_specs=[local, local, local],
        out_specs=(anywhere, anywhere),
        scratch_shapes=[
            pltpu.VMEM(shape, bf16),
            pltpu.VMEM(shape, bf16),
            dma((blocks,)),
            dma((blocks,)),
        ],
    )(
        pltpu.with_memory_space_constraint(total, pltpu.VMEM),
        pltpu.with_memory_space_constraint(scale, pltpu.VMEM),
        pltpu.with_memory_space_constraint(columns, pltpu.VMEM),
    )
    return mixed.reshape(chans, width), normed.reshape(chans, width)


def choose(out_gate, key_proj, *rest):
    chans, width = key_proj.shape
    blocks = lax.axis_size("seq")
    tiled = blocks & (blocks - 1) == 0 and chans % (blocks * WHOLE * 16) == 0 and width % 128 == 0 and blocks <= 16
    return (with_kernel if tiled else on_device)(out_gate, key_proj, *rest)


def solution(mesh):
    return jax.shard_map(
        choose,
        mesh=mesh,
        in_specs=(
            P("ch", "seq"),
            P("ch", "seq"),
            P("ch", "seq"),
            P("ch", "seq"),
            P("ch"),
            P("ch", "seq"),
            P("ch"),
        ),
        out_specs=(P("ch", "seq"), P("ch", "seq")),
        check_vma=False,
    )
```
